128 devices in a mesh: seq: 8 (over z, core), exp: 16 (over x, y).
Axes of the slice: x: 4, y: 4, z: 4, core: 2. Of those that a mesh axis runs over, the one named last changes fastest.
Arguments:
- residual: bfloat16 [16384, 8192], P(('seq', 'exp')), may hold values from -6 to 6
- expert_rows: bfloat16 [8, 16, 16, 24, 8192], P('seq', 'exp'), may hold values from -6 to 6
- expert_ids: int32 [16384, 2], P(('seq', 'exp')), may hold values from 0 to 15, as said below
- expert_slots: int32 [16384, 2], P(('seq', 'exp')), may hold values from 0 to 23, as said below
- combine_weights: float32 [16384, 2], P(('seq', 'exp')), may hold values from 0.1 to 0.9
- norm_gain: float32 [8192], replicated, may hold values from 0.1 to 1.9
- in_weight: bfloat16 [8192, 8192], P(None, 'exp'), may hold values from -0.0625 to 0.0625
- conv_weight: float32 [4, 8192], P(None, 'exp'), may hold values from -3 to 3
- conv_bias: float32 [8192], P('exp'), may hold values from -0.5 to 0.5
- bc_weight: bfloat16 [8192, 128], P('exp'), may hold values from -0.00390625 to 0.00390625
- dt_weight: bfloat16 [8192, 128], P('exp'), may hold values from -0.0625 to 0.0625
- dt_bias: float32 [128], P('exp'), may hold values from -2 to 0.5
- decay_log: float32 [128], P('exp'), may hold values from -14 to -3.2
- skip_gain: float32 [128], P('exp'), may hold values from -1 to 3
Outputs:
- scan_output: bfloat16 [16384, 8192], P('seq', 'exp')
The draws below stay inside these ranges and needn't reach their ends.
Inputs may be any that keep to these rules, and one draw needn't show every extreme that they name: `expert_ids`: A token's two ids differ. The tokens of one device name no expert more than 24 times, and in each span one expert is named exactly 24 times by the tokens of every device of the span. `expert_slots`: A token's slot at its k-th expert counts the earlier (token, k) pairs of the same device, in row-major order, that name the same expert.
All inputs are finite; a program needn't handle non-finite values.
Results may differ from the reference program's by a relative error of at most 0.0074.
Values may be sent and summed in bfloat16 or wider, within the bound.
No kernel may reach another device: no remote copies, remote signals or barrier semaphores. Data moves between devices by JAX's collectives and lax.ppermute only.
A program may use at most 320 MiB of HBM per device.

```python
import jax
import jax.numpy as jnp
from jax import lax

D = 8192
TOPK = 2
KCONV = 4
EXPERTS = 16
CH = 8192
HEAD = 64
NSTATE = 64
HEADS = 128
STRETCH = 256
TOK_DEV = 128
CAP = 24
TOKENS = 16384
N_SEQ = 8
N_EXP = 16


def routing_tables(key):
    base_key = jax.random.fold_in(key, 11)
    owners = TOKENS // TOK_DEV
    others = EXPERTS - 1
    remaining = TOPK * TOK_DEV - CAP
    base_load = remaining // others
    extra_count = remaining % others
    pair_count = others // 2
    full_key, owner_key = jax.random.split(base_key)
    full_expert = jax.random.randint(full_key, (owners // N_EXP,), 0, EXPERTS)

    def one_owner(single_key, favored):
        sub_keys = jax.random.split(single_key, 4)
        ordering = jax.random.permutation(sub_keys[0], others)
        chosen = (favored + 1 + ordering) % EXPERTS
        load_sizes = base_load + (jnp.arange(others) < extra_count).astype(jnp.int32)
        shifts = jax.random.randint(sub_keys[1], (pair_count,), 0, base_load // 3 + 1)
        load_sizes = load_sizes.at[2 * jnp.arange(pair_count)].add(shifts)
        load_sizes = load_sizes.at[2 * jnp.arange(pair_count) + 1].add(-shifts)
        counts = jnp.zeros((EXPERTS,), jnp.int32).at[chosen].set(load_sizes).at[favored].set(CAP)
        labels = jnp.repeat(jnp.arange(EXPERTS, dtype=jnp.int32), counts, total_repeat_length=TOPK * TOK_DEV)
        grouped = labels.reshape(TOPK, TOK_DEV).T
        shuffled = grouped[jax.random.permutation(sub_keys[2], TOK_DEV)]
        flipped = jax.random.randint(sub_keys[3], (TOK_DEV,), 0, 2) == 1
        routed = jnp.where(flipped[:, None], shuffled[:, ::-1], shuffled)
        flat_ids = routed.reshape(-1)
        onehot = (flat_ids[:, None] == jnp.arange(EXPERTS, dtype=jnp.int32)[None, :]).astype(jnp.int32)
        before = jnp.cumsum(onehot, axis=0) - onehot
        slot_index = jnp.sum(before * onehot, axis=1).reshape(TOK_DEV, TOPK)
        return (routed, slot_index)
    favored_each = jnp.repeat(full_expert, N_EXP)
    routed, slot_index = jax.vmap(one_owner)(jax.random.split(owner_key, owners), favored_each)
    return (routed.reshape(TOKENS, TOPK).astype(jnp.int32), slot_index.reshape(TOKENS, TOPK).astype(jnp.int32))


def draw_expert_ids(key, part):
    return routing_tables(key)[0]


def draw_expert_slots(key, part):
    return routing_tables(key)[1]


def draw_decay_log(key, part):
    return jax.random.uniform(key, (HEADS,), jnp.float32, -14.0, -3.2)


def draw_skip_gain(key, part):
    offset_key = jax.random.fold_in(jax.random.fold_in(key, 23), 1)
    return jax.random.uniform(offset_key, (HEADS,), jnp.float32, -1.0, 3.0)


def block_levels(own_key, extent, cuts, low, top_value):
    def one(position, shards_of):
        steps = jax.random.uniform(jax.random.fold_in(jax.random.fold_in(own_key, 6), position), (shards_of,), jnp.float32, low / len(cuts), top_value / len(cuts))
        return jnp.repeat(jnp.exp(steps), extent[position] // shards_of).reshape((-1,) + (1,) * (len(extent) - position - 1))

    level = one(*cuts[0])
    for cut in cuts[1:]:
        level = level * one(*cut)
    return level


def normal_values(stream_key, shape, width, bound, pieces=(), held_as=jnp.bfloat16):
    values = width * jax.random.normal(stream_key, shape, jnp.float32)
    if pieces:
        values = values * block_levels(stream_key, shape, pieces, -0.22, 0.18)
    return jnp.clip(values, -bound, bound).astype(held_as)


def setup_inputs(seed: int = 0) -> dict:
    key_list = jax.random.split(jax.random.key(seed), 15)
    residual = normal_values(key_list[0], (TOKENS, D), 1.0, 6.0, ((0, 128),))
    expert_rows = normal_values(key_list[1], (N_SEQ, EXPERTS, N_EXP, CAP, D), 1.0, 6.0, ((0, 8), (1, 16)))
    expert_ids = draw_expert_ids(jax.random.fold_in(key_list[14], 71), 0)
    expert_slots = draw_expert_slots(jax.random.fold_in(key_list[14], 71), 0)
    combine_weights = jnp.clip(0.1 + 0.79999997 * jax.random.uniform(key_list[4], (TOKENS, TOPK), jnp.float32) ** block_levels(key_list[4], (TOKENS, TOPK), ((0, 128),), -0.2, 0.2), 0.1, 0.9)
    norm_gain = jnp.clip(1.0 + 0.18 * jax.random.normal(key_list[5], (D,), jnp.float32), 0.1, 1.9)
    in_weight = normal_values(key_list[6], (D, CH), D ** -0.5, 0.0625, ((1, 16),))
    conv_weight = normal_values(key_list[7], (KCONV, CH), 0.6, 3.0, ((1, 16),), jnp.float32)
    conv_bias = jnp.clip(jax.random.uniform(key_list[8], (CH,), jnp.float32, -0.5, 0.5) * block_levels(key_list[8], (CH,), ((0, 16),), -0.4, 0.0), -0.5, 0.5)
    bc_weight = normal_values(key_list[9], (CH, 2 * NSTATE), (CH * 256) ** -0.5, 0.00390625, ((0, 16),))
    dt_weight = normal_values(key_list[10], (CH, HEADS), CH ** -0.5, 0.0625, ((0, 16),))
    dt_bias = jnp.clip(-2.0 + 2.5 * jax.random.uniform(key_list[11], (HEADS,), jnp.float32) ** block_levels(key_list[11], (HEADS,), ((0, 16),), -0.2, 0.2), -2.0, 0.5)
    decay_log = draw_decay_log(jax.random.fold_in(key_list[14], 71), 0)
    skip_gain = draw_skip_gain(jax.random.fold_in(key_list[14], 71), 0)
    return dict(residual=residual, expert_rows=expert_rows, expert_ids=expert_ids, expert_slots=expert_slots, combine_weights=combine_weights, norm_gain=norm_gain, in_weight=in_weight, conv_weight=conv_weight, conv_bias=conv_bias, bc_weight=bc_weight, dt_weight=dt_weight, dt_bias=dt_bias, decay_log=decay_log, skip_gain=skip_gain)


def block_terms(b_rows, c_rows, steps_dt, decays, values):
    running = jnp.cumsum(decays, axis=0)
    scores = jnp.dot(c_rows, b_rows.T, preferred_element_type=jnp.float32)
    length = running.shape[0]
    causal = (jnp.arange(length)[:, None] >= jnp.arange(length)[None, :])[:, :, None]
    decay_gap = jnp.where(causal, running[:, None, :] - running[None, :, :], 0.0)
    mixing = jnp.where(causal, jnp.exp(decay_gap) * scores[:, :, None] * steps_dt[None, :, :], 0.0).astype(jnp.bfloat16)
    inside = jnp.einsum('tsh,shp->thp', mixing.astype(jnp.float32), values.astype(jnp.float32))
    carried = jnp.exp(running[-1][None, :] - running) * steps_dt
    states = jnp.einsum('sn,shp->hnp', b_rows.astype(jnp.float32), carried[:, :, None] * values.astype(jnp.float32), precision=lax.Precision.HIGHEST)
    return (running, inside, states, jnp.exp(running[-1]))

def reference(residual, expert_rows, expert_ids, expert_slots, combine_weights, norm_gain, in_weight, conv_weight, conv_bias, bc_weight, dt_weight, dt_bias, decay_log, skip_gain):
    owners = N_SEQ * N_EXP

    def combine_owner(inputs):
        owner, resid_rows, owner_ids, owner_slots, owner_weights = inputs
        buffers = expert_rows[owner // N_EXP, :, owner % N_EXP].reshape(EXPERTS * CAP, D)
        picked = buffers[owner_ids * CAP + owner_slots]
        mixture = jnp.zeros((TOK_DEV, D), jnp.float32)
        for column in range(TOPK):
            mixture = mixture + owner_weights[:, column][:, None] * picked[:, column].astype(jnp.float32)
        stream = resid_rows.astype(jnp.float32) + mixture
        factor = lax.rsqrt(lax.optimization_barrier(jnp.mean(stream * stream, axis=1, keepdims=True)) + 1e-06)
        return (stream * factor * norm_gain[None, :]).astype(jnp.bfloat16)
    normed = lax.map(combine_owner, (jnp.arange(owners, dtype=jnp.int32), residual.reshape(owners, TOK_DEV, D), expert_ids.reshape(owners, TOK_DEV, TOPK), expert_slots.reshape(owners, TOK_DEV, TOPK), combine_weights.reshape(owners, TOK_DEV, TOPK))).reshape(TOKENS, D)
    x_in = jnp.dot(normed, in_weight, preferred_element_type=jnp.float32).astype(jnp.bfloat16)
    padded = jnp.concatenate([jnp.zeros((KCONV - 1, CH), jnp.bfloat16), x_in], axis=0)
    filtered = jnp.zeros((TOKENS, CH), jnp.float32) + conv_bias[None, :]
    for tap in range(KCONV):
        filtered = filtered + conv_weight[tap][None, :] * padded[tap:tap + TOKENS].astype(jnp.float32)
    activated = jax.nn.silu(filtered).astype(jnp.bfloat16)
    state_proj = jnp.dot(activated, bc_weight, preferred_element_type=jnp.float32)
    dt_raw = jnp.dot(activated, dt_weight, preferred_element_type=jnp.float32)
    b_all = state_proj[:, :NSTATE].astype(jnp.bfloat16)
    c_all = state_proj[:, NSTATE:].astype(jnp.bfloat16)
    steps_dt = jax.nn.softplus(dt_raw + dt_bias[None, :])
    decays = -jnp.exp(decay_log)[None, :] * steps_dt
    blocks = TOKENS // STRETCH

    def advance(carried_states, inputs):
        b_rows, c_rows, block_dt, block_decays, values = inputs
        running, inside, states, total = block_terms(b_rows, c_rows, block_dt, block_decays, values)
        across = jnp.exp(running)[:, :, None] * jnp.einsum('tn,hnp->thp', c_rows.astype(jnp.float32), carried_states, precision=lax.Precision.HIGHEST)
        output = inside + across + skip_gain[None, :, None] * values.astype(jnp.float32)
        return (total[:, None, None] * carried_states + states, output.astype(jnp.bfloat16))
    final_states, outputs = lax.scan(advance, jnp.zeros((HEADS, NSTATE, HEAD), jnp.float32), (b_all.reshape(blocks, STRETCH, NSTATE), c_all.reshape(blocks, STRETCH, NSTATE), steps_dt.reshape(blocks, STRETCH, HEADS), decays.reshape(blocks, STRETCH, HEADS), activated.reshape(blocks, STRETCH, HEADS, HEAD)))
    return outputs.reshape(TOKENS, CH)
```

```python
import jax
import jax.numpy as jnp
from jax import lax
from jax.experimental import pallas as pl
from jax.experimental.pallas import tpu as pltpu
from jax.sharding import Mesh, PartitionSpec as P

TOPK = 2
KCONV = 4
HEAD = 64
NSTATE = 64
STRETCH = 256
EPS = 1e-06
SPAN = ("z", "c")
PLANE = ("x", "y")
BF16 = jnp.bfloat16
F32 = jnp.float32
EXACT = lax.Precision.HIGHEST


def shifted(value, axis, steps):
    count = lax.axis_size(axis)
    return lax.ppermute(value, axis, [(i, (i + steps) % count) for i in range(count)])


def passed_on(value, axes, steps):
    count = lax.axis_size(axes)
    return lax.ppermute(value, axes, [(i, i + steps) for i in range(count - steps)])


def whole(shape):
    return pl.BlockSpec(shape, lambda *_: (0,) * len(shape))


def dot(a, b, dims=((1,), (0,)), precision=None):
    return lax.dot_general(a, b, (dims, ((), ())), precision=precision, preferred_element_type=F32)


def combine_body(index_ref, weight_ref, rows_ref, residual_ref, gain_ref, out_ref, stream_ref):
    own, width = residual_ref.shape
    slots = rows_ref.shape[0]
    step = 1024
    lane = lax.broadcasted_iota(jnp.int32, (own, slots), 1)
    mix = jnp.zeros((own, slots), F32)
    for k in range(TOPK):
        mix = mix + jnp.where(lane == index_ref[:, k : k + 1], weight_ref[:, k : k + 1], 0.0)
    high = mix.astype(BF16)
    low = (mix - high.astype(F32)).astype(BF16)

    def gather(i, total):
        cols = pl.ds(pl.multiple_of(i * step, step), step)
        rows = rows_ref[:, cols]
        stream = residual_ref[:, cols].astype(F32) + (dot(high, rows) + dot(low, rows))
        stream_ref[:, cols] = stream
        return total + jnp.sum(stream * stream, axis=1, keepdims=True)

    total = lax.fori_loop(0, width // step, gather, jnp.zeros((own, 1), F32))
    factor = lax.rsqrt(total / width + EPS)

    def scale(i, carry):
        cols = pl.ds(pl.multiple_of(i * step, step), step)
        out_ref[:, cols] = (stream_ref[:, cols] * factor * gain_ref[:, cols]).astype(BF16)
        return carry

    lax.fori_loop(0, width // step, scale, 0)


def combine(index, weights, rows, residual, gain):
    own, width = residual.shape
    return pl.pallas_call(
        combine_body,
        name="combine",
        out_shape=jax.ShapeDtypeStruct((own, width), BF16),
        scratch_shapes=[pltpu.VMEM((own, width), F32)],
    )(index, weights, rows, residual, gain.reshape(1, width))


def project_body(*refs):
    *x_refs, w_ref, out_ref, acc_ref = refs
    k = pl.program_id(1)
    depth = w_ref.shape[-2]
    rows = x_refs[0].shape[0]
    cols = pl.ds(pl.multiple_of(k * depth, depth), depth)
    left = jnp.concatenate([ref[:, cols] for ref in x_refs], axis=0)
    part = dot(left, w_ref[...].reshape(w_ref.shape[-2:]))

    @pl.when(k == 0)
    def _():
        acc_ref[...] = part

    @pl.when(k > 0)
    def _():
        acc_ref[...] += part

    @pl.when(k == pl.num_programs(1) - 1)
    def _():
        for u in range(len(x_refs)):
            out_ref[0, u] = acc_ref[u * rows : (u + 1) * rows].astype(BF16)


def project(units, weight, weight_spec, shards, depth_steps):
    rows, width = units[0].shape
    cols = weight.shape[-1]
    return pl.pallas_call(
        project_body,
        name="project",
        grid=(shards, depth_steps),
        in_specs=[whole((rows, width)) for _ in units] + [weight_spec],
        out_specs=pl.BlockSpec((1, len(units), rows, cols), lambda r, k: (r, 0, 0, 0)),
        out_shape=jax.ShapeDtypeStruct((shards, len(units), rows, cols), BF16),
        scratch_shapes=[pltpu.VMEM((len(units) * rows, cols), F32)],
    )(*units, weight)


def filter_body(place_ref, near_ref, far_ref, rim_ref, taps_ref, weight_ref, act_ref, part_ref, pad_ref):
    r = pl.program_id(0)
    near, rows, cols = near_ref.shape[1:]
    y = place_ref[0]
    order = (0, 1, 3)
    units = near + 1
    pad_ref[0:8] = rim_ref[0].astype(F32)
    for u in range(near):
        at = (y + order[u]) % units
        pad_ref[pl.ds(pl.multiple_of(8 + at * rows, 8), rows)] = near_ref[0, u].astype(F32)
    at = (y + 2) % units
    pad_ref[pl.ds(pl.multiple_of(8 + at * rows, 8), rows)] = far_ref[0, 0].astype(F32)
    total = units * rows
    step = 128
    for i in range(total // step):
        filtered = taps_ref[0, KCONV : KCONV + 1, :]
        for tap in range(KCONV):
            first = 8 - (KCONV - 1) + tap + i * step
            filtered = filtered + taps_ref[0, tap : tap + 1, :] * pad_ref[first : first + step]
        act_ref[0, i * step : (i + 1) * step] = jax.nn.silu(filtered).astype(BF16)
    part = dot(act_ref[0], weight_ref[0])

    @pl.when(r == 0)
    def _():
        part_ref[...] = part

    @pl.when(r > 0)
    def _():
        part_ref[...] += part


def filter_rows(y, near, far, rim, taps, weights):
    shards, n_near, rows, cols = near.shape
    total = (n_near + 1) * rows
    maps = weights.shape[-1]
    return pl.pallas_call(
        filter_body,
        name="filter",
        grid_spec=pltpu.PrefetchScalarGridSpec(
            num_scalar_prefetch=1,
            grid=(shards,),
            in_specs=[
                pl.BlockSpec((1, n_near, rows, cols), lambda r, _: (r, 0, 0, 0)),
                pl.BlockSpec((1, 1, rows, cols), lambda r, _: (r, 0, 0, 0)),
                pl.BlockSpec((1, 8, cols), lambda r, _: (r, 0, 0)),
                pl.BlockSpec((1, 8, cols), lambda r, _: (r, 0, 0)),
                pl.BlockSpec((1, cols, maps), lambda r, _: (r, 0, 0)),
            ],
            out_specs=[
                pl.BlockSpec((1, total, cols), lambda r, _: (r, 0, 0)),
                pl.BlockSpec((total, maps), lambda r, _: (0, 0)),
            ],
            scratch_shapes=[pltpu.VMEM((total + 8, cols), F32)],
        ),
        out_shape=[
            jax.ShapeDtypeStruct((shards, total, cols), BF16),
            jax.ShapeDtypeStruct((total, maps), F32),
        ],
    )(y.reshape(1), near, far, rim, taps, weights)


def wide(narrow, spread):
    return dot(narrow, spread, precision=EXACT)


def rates_of(rate_rows, choice, head_row):
    raw = wide(rate_rows, choice)
    step = jax.nn.softplus(raw + head_row[0:1])
    return step, -jnp.exp(head_row[1:2]) * step


def lower(n):
    return (
        lax.broadcasted_iota(jnp.int32, (n, n), 0) >= lax.broadcasted_iota(jnp.int32, (n, n), 1)
    ).astype(F32)


def state_body(place_ref, maps_ref, act_ref, choice_ref, spread_ref, head_ref, start_ref, run_ref, final_ref, state_ref, sum_ref):
    b = pl.program_id(0)
    n = act_ref.shape[1]

    @pl.when(b == 0)
    def _():
        state_ref[...] = jnp.zeros_like(state_ref)
        sum_ref[...] = jnp.zeros_like(sum_ref)

    maps = maps_ref[...].reshape(n, maps_ref.shape[-1])
    step, decay = rates_of(maps[:, 2 * NSTATE :], choice_ref[...], head_ref[...])
    running = dot(lower(n), decay, precision=EXACT)
    total = running[n - 1 : n]
    spread = spread_ref[...]
    carried = wide(jnp.exp(total - running) * step, spread) * act_ref[0].astype(F32)
    high = carried.astype(BF16)
    low = (carried - high.astype(F32)).astype(BF16)
    b_rows = maps[:, :NSTATE].astype(BF16)
    state = dot(b_rows, high, ((0,), (0,))) + dot(b_rows, low, ((0,), (0,)))
    run_ref[...] = sum_ref[0:1] + running
    start_ref[0] = state_ref[...]
    state_ref[...] = wide(jnp.broadcast_to(jnp.exp(total), (8, total.shape[1])), spread)[0:1] * state_ref[...] + state
    sum_ref[...] = sum_ref[...] + total

    @pl.when(b == pl.num_programs(0) - 1)
    def _():
        final_ref[0:NSTATE] = state_ref[...]
        final_ref[NSTATE : NSTATE + 8] = wide(jnp.exp(sum_ref[...]), spread)


def inside_body(place_ref, maps_ref, act_ref, choice_ref, choice_t_ref, spread_ref, head_ref, head_t_ref, skip_ref, start_ref, out_ref):
    n = act_ref.shape[1]
    half = n // 2
    maps = maps_ref[...].reshape(n, maps_ref.shape[-1])
    rates = maps[:, 2 * NSTATE :]
    step, decay = rates_of(rates, choice_ref[...], head_ref[...])
    tri = lower(n)
    running = dot(tri, decay, precision=EXACT)
    raw_t = dot(choice_t_ref[...], rates, ((1,), (1,)), precision=EXACT)
    step_t = jax.nn.softplus(raw_t + head_t_ref[:, 0:1])
    decay_t = -jnp.exp(head_t_ref[:, 1:2]) * step_t
    running_t = dot(decay_t, tri, ((1,), (1,)), precision=EXACT)
    b_rows = maps[:, :NSTATE].astype(BF16)
    c_rows = maps[:, NSTATE : 2 * NSTATE].astype(BF16)
    scores = tri * dot(c_rows, b_rows, ((1,), (1,)))
    start = start_ref[0]
    high = start.astype(BF16)
    low = (start - high.astype(F32)).astype(BF16)
    across = dot(c_rows, high) + dot(c_rows, low)
    act = act_ref[0]
    base = wide(jnp.exp(running), spread_ref[...]) * across + skip_ref[...] * act.astype(F32)
    heads = act.shape[1] // HEAD
    first = lax.broadcasted_iota(jnp.int32, (1, 2 * HEAD), 1) < HEAD
    for pair in range(heads // 2):
        cols = slice(2 * HEAD * pair, 2 * HEAD * (pair + 1))
        values = act[:, cols]
        tops, bottoms = [], []
        for h in (2 * pair, 2 * pair + 1):
            row, gain = running_t[h : h + 1], step_t[h : h + 1]
            column = running[:, h : h + 1]
            top = jnp.exp(jnp.minimum(column[:half] - row[:, :half], 0.0)) * scores[:half, :half] * gain[:, :half]
            bottom = jnp.exp(jnp.minimum(column[half:] - row, 0.0)) * scores[half:] * gain
            tops.append(dot(top.astype(BF16), values[:half]))
            bottoms.append(dot(bottom.astype(BF16), values))
        out_ref[:half, cols] = base[:half, cols] + jnp.where(first, tops[0], tops[1])
        out_ref[half:, cols] = base[half:, cols] + jnp.where(first, bottoms[0], bottoms[1])


def finish_body(inside_ref, maps_ref, run_ref, spread_ref, entering_ref, out_ref):
    n = inside_ref.shape[0]
    maps = maps_ref[...].reshape(n, maps_ref.shape[-1])
    c_rows = maps[:, NSTATE : 2 * NSTATE].astype(BF16)
    entering = entering_ref[...]
    high = entering.astype(BF16)
    low = (entering - high.astype(F32)).astype(BF16)
    across = dot(c_rows, high) + dot(c_rows, low)
    out_ref[...] = (inside_ref[...] + wide(jnp.exp(run_ref[...]), spread_ref[...]) * across).astype(BF16)


def scan_output(x, maps, act, dt_bias, decay_log, skip_gain, e):
    subs, rows, cols = act.shape
    tokens = subs * rows
    blocks = tokens // STRETCH
    inner = rows // STRETCH
    heads = cols // HEAD
    n_maps = maps.shape[1]
    lanes = n_maps - 2 * NSTATE
    head = lax.broadcasted_iota(jnp.int32, (lanes, lanes), 0)
    lane = lax.broadcasted_iota(jnp.int32, (lanes, lanes), 1)
    choice = ((head == lane + e * heads) & (lane < heads)).astype(F32)
    choice_t = (
        lax.broadcasted_iota(jnp.int32, (heads, lanes), 1)
        == lax.broadcasted_iota(jnp.int32, (heads, lanes), 0) + e * heads
    ).astype(F32)
    spread = (
        lax.broadcasted_iota(jnp.int32, (lanes, cols), 0)
        == lax.broadcasted_iota(jnp.int32, (lanes, cols), 1) // HEAD
    ).astype(F32)
    per_head = jnp.stack([dt_bias, decay_log])
    head_row = jnp.pad(per_head, ((0, 6), (0, lanes - heads)))
    head_t = jnp.pad(per_head.T, ((0, 0), (0, lanes - 2)))
    skip = jnp.repeat(skip_gain, HEAD)[None, :]
    place = x.reshape(1)

    maps_spec = pl.BlockSpec((STRETCH, n_maps), lambda b, *_: (b, 0))
    act_spec = pl.BlockSpec((1, STRETCH, cols), lambda b, p: ((p[0] + subs - b // inner) % subs, b % inner, 0))
    start_spec = pl.BlockSpec((1, NSTATE, cols), lambda b, *_: (b, 0, 0))
    lane_spec = pl.BlockSpec((STRETCH, lanes), lambda b, *_: (b, 0))
    wide_spec = pl.BlockSpec((STRETCH, cols), lambda b, *_: (b, 0))
    start, runs, final = pl.pallas_call(
        state_body,
        name="states",
        grid_spec=pltpu.PrefetchScalarGridSpec(
            num_scalar_prefetch=1,
            grid=(blocks,),
            in_specs=[maps_spec, act_spec, whole((lanes, lanes)), whole((lanes, cols)), whole((8, lanes))],
            out_specs=[start_spec, lane_spec, whole((NSTATE + 8, cols))],
            scratch_shapes=[pltpu.VMEM((NSTATE, cols), F32), pltpu.VMEM((8, lanes), F32)],
        ),
        out_shape=[
            jax.ShapeDtypeStruct((blocks, NSTATE, cols), F32),
            jax.ShapeDtypeStruct((tokens, lanes), F32),
            jax.ShapeDtypeStruct((NSTATE + 8, cols), F32),
        ],
    )(place, maps, act, choice, spread, head_row)

    gone = [passed_on(final, SPAN, d) for d in range(1, lax.axis_size(SPAN))]

    inside = pl.pallas_call(
        inside_body,
        name="inside",
        grid_spec=pltpu.PrefetchScalarGridSpec(
            num_scalar_prefetch=1,
            grid=(blocks,),
            in_specs=[
                maps_spec,
                act_spec,
                whole((lanes, lanes)),
                whole((heads, lanes)),
                whole((lanes, cols)),
                whole((8, lanes)),
                whole((heads, lanes)),
                whole((1, cols)),
                start_spec,
            ],
            out_specs=wide_spec,
        ),
        out_shape=jax.ShapeDtypeStruct((tokens, cols), F32),
    )(place, maps, act, choice, choice_t, spread, head_row, head_t, skip, start)

    entering = gone[0][:NSTATE]
    decay = gone[0][NSTATE : NSTATE + 1]
    for block in gone[1:]:
        entering = entering + decay * block[:NSTATE]
        decay = decay * block[NSTATE : NSTATE + 1]

    return pl.pallas_call(
        finish_body,
        name="finish",
        grid=(blocks,),
        in_specs=[wide_spec, maps_spec, lane_spec, whole((lanes, cols)), whole((NSTATE, cols))],
        out_specs=wide_spec,
        out_shape=jax.ShapeDtypeStruct((tokens, cols), BF16),
    )(inside, maps, runs, spread, entering)


def shards(
    residual,
    expert_rows,
    expert_ids,
    expert_slots,
    combine_weights,
    norm_gain,
    in_weight,
    conv_weight,
    conv_bias,
    bc_weight,
    dt_weight,
    dt_bias,
    decay_log,
    skip_gain,
):
    own, width = residual.shape
    spans = lax.axis_size(SPAN)
    nx, ny = lax.axis_size("x"), lax.axis_size("y")
    s, e, x, y = (lax.axis_index(axis) for axis in (SPAN, PLANE, "x", "y"))
    local = in_weight.shape[1]
    depth = width // spans

    piece = lax.dynamic_slice_in_dim(in_weight, s * depth, depth, 0)
    pieces = [shifted(piece, "x", -r) for r in range(1, nx)]
    maps_weight = jnp.concatenate([bc_weight, dt_weight], axis=1)
    taps = jnp.concatenate([conv_weight, conv_bias[None], jnp.zeros((7 - KCONV, local), F32)], axis=0)
    maps_weights = jnp.stack([maps_weight] + [shifted(maps_weight, "x", -r) for r in range(1, nx)])
    all_taps = jnp.stack([taps] + [shifted(taps, "x", -r) for r in range(1, nx)])
    others = lax.all_gather(jnp.stack(pieces), SPAN)

    returned = lax.all_to_all(expert_rows, PLANE, split_axis=2, concat_axis=1, tiled=True)
    capacity = returned.shape[3]
    rows = returned.reshape(returned.shape[1] * capacity, width)
    normed = combine(expert_ids * capacity + expert_slots, combine_weights, rows, residual, norm_gain)

    below = shifted(normed, "y", 1)
    above = shifted(normed, "y", -1)
    half = own // 2
    far = jnp.concatenate([shifted(below[:half], "y", 1), shifted(above[half:], "y", -1)], axis=0)

    own_spec = pl.BlockSpec((depth, local), lambda r, k: (k, 0))
    other_spec = pl.BlockSpec((1, 1, depth, local), lambda r, k: (k, r, 0, 0))
    near = (normed, above, below)
    near_in = jnp.concatenate(
        [project(near, in_weight, own_spec, 1, spans), project(near, others, other_spec, nx - 1, spans)], axis=0
    )
    far_in = jnp.concatenate(
        [project((far,), in_weight, own_spec, 1, spans), project((far,), others, other_spec, nx - 1, spans)], axis=0
    )

    ends = jnp.stack([near_in[:, 0, -8:], near_in[:, 1, -8:], far_in[:, 0, -8:], near_in[:, 2, -8:]], axis=0)
    last = lax.dynamic_index_in_dim(ends, (ny - 1 - y) % ny, 0, keepdims=False)
    rim = passed_on(jnp.roll(last, -1, axis=0), SPAN + ("x",), 1)
    act, part = filter_rows(y, near_in, far_in, rim, all_taps, maps_weights)

    act_here = jnp.stack([act[0]] + [shifted(act[r], "x", r) for r in range(1, nx)])

    part = part.reshape(ny, own, part.shape[1])
    mine = lax.dynamic_index_in_dim(part, y, 0, keepdims=False)
    for d in range(1, ny):
        mine = mine + shifted(lax.dynamic_index_in_dim(part, (y + d) % ny, 0, keepdims=False), "y", d)
    maps = lax.all_gather(mine, PLANE, axis=0, tiled=True)
    return scan_output(x, maps, act_here, dt_bias, decay_log, skip_gain, e)


def solution(mesh):
    spans, plane = mesh.devices.shape
    side = 4
    fine = Mesh(mesh.devices.reshape(spans // 2, 2, plane // side, side), ("z", "c", "x", "y"))
    placed = (
        P(("z", "c", "x", "y"), None),
        P(SPAN, PLANE, None, None, None),
        P(("z", "c", "x", "y"), None),
        P(("z", "c", "x", "y"), None),
        P(("z", "c", "x", "y"), None),
        P(),
        P(None, PLANE),
        P(None, PLANE),
        P(PLANE),
        P(PLANE, None),
        P(PLANE, None),
        P(PLANE),
        P(PLANE),
        P(PLANE),
    )
    return jax.shard_map(shards, mesh=fine, in_specs=placed, out_specs=P(SPAN, PLANE), check_vma=False)
```

```python
import jax
import jax.numpy as jnp
from jax import lax
from jax.experimental import pallas as pl
from jax.experimental.pallas import tpu as pltpu
from jax.sharding import Mesh, PartitionSpec as P

TOPK = 2
KCONV = 4
HEAD = 64
NSTATE = 64
STRETCH = 256
EPS = 1e-06
SPAN = ("z", "c")
PLANE = ("x", "y")
BF16 = jnp.bfloat16
F32 = jnp.float32
EXACT = lax.Precision.HIGHEST


def shifted(value, axis, steps):
    count = lax.axis_size(axis)
    return lax.ppermute(value, axis, [(i, (i + steps) % count) for i in range(count)])


def passed_on(value, axes, steps):
    count = lax.axis_size(axes)
    return lax.ppermute(value, axes, [(i, i + steps) for i in range(count - steps)])


def whole(shape):
    return pl.BlockSpec(shape, lambda *_: (0,) * len(shape))


def dot(a, b, dims=((1,), (0,)), precision=None):
    return lax.dot_general(a, b, (dims, ((), ())), precision=precision, preferred_element_type=F32)


def combine_body(index_ref, weight_ref, rows_ref, residual_ref, gain_ref, out_ref, stream_ref):
    own, width = residual_ref.shape
    slots = rows_ref.shape[0]
    step = 1024
    lane = lax.broadcasted_iota(jnp.int32, (own, slots), 1)
    mix = jnp.zeros((own, slots), F32)
    for k in range(TOPK):
        mix = mix + jnp.where(lane == index_ref[:, k : k + 1], weight_ref[:, k : k + 1], 0.0)
    high = mix.astype(BF16)
    low = (mix - high.astype(F32)).astype(BF16)

    def gather(i, total):
        cols = pl.ds(pl.multiple_of(i * step, step), step)
        rows = rows_ref[:, cols]
        stream = residual_ref[:, cols].astype(F32) + (dot(high, rows) + dot(low, rows))
        stream_ref[:, cols] = stream
        return total + jnp.sum(stream * stream, axis=1, keepdims=True)

    total = lax.fori_loop(0, width // step, gather, jnp.zeros((own, 1), F32))
    factor = lax.rsqrt(total / width + EPS)

    def scale(i, carry):
        cols = pl.ds(pl.multiple_of(i * step, step), step)
        out_ref[:, cols] = (stream_ref[:, cols] * factor * gain_ref[:, cols]).astype(BF16)
        return carry

    lax.fori_loop(0, width // step, scale, 0)


def combine(index, weights, rows, residual, gain):
    own, width = residual.shape
    return pl.pallas_call(
        combine_body,
        name="combine",
        out_shape=jax.ShapeDtypeStruct((own, width), BF16),
        scratch_shapes=[pltpu.VMEM((own, width), F32)],
    )(index, weights, rows, residual, gain.reshape(1, width))


def project_body(*refs):
    _, *x_refs, w_ref, out_ref, acc_ref = refs
    k = pl.program_id(1)
    weight = w_ref[...].reshape(-1, w_ref.shape[-1])
    depth = weight.shape[0]
    rows = x_refs[0].shape[0]
    cols = pl.ds(pl.multiple_of(k * depth, depth), depth)
    left = jnp.concatenate([ref[:, cols] for ref in x_refs], axis=0)
    part = dot(left, weight)

    @pl.when(k == 0)
    def _():
        acc_ref[...] = part

    @pl.when(k > 0)
    def _():
        acc_ref[...] += part

    @pl.when(k == pl.num_programs(1) - 1)
    def _():
        for u in range(len(x_refs)):
            out_ref[0, u] = acc_ref[u * rows : (u + 1) * rows].astype(BF16)


def project(place, units, weight, weight_spec, shards, depth_steps):
    rows, width = units[0].shape
    cols = weight.shape[-1]
    return pl.pallas_call(
        project_body,
        name="project",
        grid_spec=pltpu.PrefetchScalarGridSpec(
            num_scalar_prefetch=1,
            grid=(shards, depth_steps),
            in_specs=[whole((rows, width)) for _ in units] + [weight_spec],
            out_specs=pl.BlockSpec((1, len(units), rows, cols), lambda r, k, _: (r, 0, 0, 0)),
            scratch_shapes=[pltpu.VMEM((len(units) * rows, cols), F32)],
        ),
        out_shape=jax.ShapeDtypeStruct((shards, len(units), rows, cols), BF16),
    )(place.reshape(1), *units, weight)


def filter_body(place_ref, near_ref, far_ref, rim_ref, taps_ref, weight_ref, act_ref, part_ref, pad_ref):
    r = pl.program_id(0)
    near, rows, cols = near_ref.shape[1:]
    y = place_ref[0]
    order = (0, 1, 3)
    units = near + 1
    pad_ref[0:8] = rim_ref[0].astype(F32)
    for u in range(near):
        at = (y + order[u]) % units
        pad_ref[pl.ds(pl.multiple_of(8 + at * rows, 8), rows)] = near_ref[0, u].astype(F32)
    at = (y + 2) % units
    pad_ref[pl.ds(pl.multiple_of(8 + at * rows, 8), rows)] = far_ref[0, 0].astype(F32)
    total = units * rows
    step = 128
    for i in range(total // step):
        filtered = taps_ref[0, KCONV : KCONV + 1, :]
        for tap in range(KCONV):
            first = 8 - (KCONV - 1) + tap + i * step
            filtered = filtered + taps_ref[0, tap : tap + 1, :] * pad_ref[first : first + step]
        act_ref[0, i * step : (i + 1) * step] = jax.nn.silu(filtered).astype(BF16)
    part = dot(act_ref[0], weight_ref[0])

    @pl.when(r == 0)
    def _():
        part_ref[...] = part

    @pl.when(r > 0)
    def _():
        part_ref[...] += part


def filter_rows(y, near, far, rim, taps, weights):
    shards, n_near, rows, cols = near.shape
    total = (n_near + 1) * rows
    maps = weights.shape[-1]
    return pl.pallas_call(
        filter_body,
        name="filter",
        grid_spec=pltpu.PrefetchScalarGridSpec(
            num_scalar_prefetch=1,
            grid=(shards,),
            in_specs=[
                pl.BlockSpec((1, n_near, rows, cols), lambda r, _: (r, 0, 0, 0)),
                pl.BlockSpec((1, 1, rows, cols), lambda r, _: (r, 0, 0, 0)),
                pl.BlockSpec((1, 8, cols), lambda r, _: (r, 0, 0)),
                pl.BlockSpec((1, 8, cols), lambda r, _: (r, 0, 0)),
                pl.BlockSpec((1, cols, maps), lambda r, _: (r, 0, 0)),
            ],
            out_specs=[
                pl.BlockSpec((1, total, cols), lambda r, _: (r, 0, 0)),
                pl.BlockSpec((total, maps), lambda r, _: (0, 0)),
            ],
            scratch_shapes=[pltpu.VMEM((total + 8, cols), F32)],
        ),
        out_shape=[
            jax.ShapeDtypeStruct((shards, total, cols), BF16),
            jax.ShapeDtypeStruct((total, maps), F32),
        ],
    )(y.reshape(1), near, far, rim, taps, weights)


def wide(narrow, spread):
    return dot(narrow, spread, precision=EXACT)


def rates_of(rate_rows, choice, head_row):
    raw = wide(rate_rows, choice)
    step = jax.nn.softplus(raw + head_row[0:1])
    return step, -jnp.exp(head_row[1:2]) * step


def lower(n):
    return (
        lax.broadcasted_iota(jnp.int32, (n, n), 0) >= lax.broadcasted_iota(jnp.int32, (n, n), 1)
    ).astype(F32)


def state_body(place_ref, maps_ref, act_ref, choice_ref, spread_ref, head_ref, start_ref, run_ref, final_ref, state_ref, sum_ref):
    b = pl.program_id(0)
    n = act_ref.shape[1]

    @pl.when(b == 0)
    def _():
        state_ref[...] = jnp.zeros_like(state_ref)
        sum_ref[...] = jnp.zeros_like(sum_ref)

    maps = maps_ref[...].reshape(n, maps_ref.shape[-1])
    step, decay = rates_of(maps[:, 2 * NSTATE :], choice_ref[...], head_ref[...])
    running = dot(lower(n), decay, precision=EXACT)
    total = running[n - 1 : n]
    spread = spread_ref[...]
    carried = wide(jnp.exp(total - running) * step, spread) * act_ref[0].astype(F32)
    high = carried.astype(BF16)
    low = (carried - high.astype(F32)).astype(BF16)
    b_rows = maps[:, :NSTATE].astype(BF16)
    state = dot(b_rows, high, ((0,), (0,))) + dot(b_rows, low, ((0,), (0,)))
    run_ref[...] = sum_ref[0:1] + running
    start_ref[0] = state_ref[...]
    state_ref[...] = wide(jnp.broadcast_to(jnp.exp(total), (8, total.shape[1])), spread)[0:1] * state_ref[...] + state
    sum_ref[...] = sum_ref[...] + total

    @pl.when(b == pl.num_programs(0) - 1)
    def _():
        final_ref[0:NSTATE] = state_ref[...]
        final_ref[NSTATE : NSTATE + 8] = wide(jnp.exp(sum_ref[...]), spread)


def inside_body(place_ref, maps_ref, act_ref, choice_ref, choice_t_ref, spread_ref, head_ref, head_t_ref, skip_ref, start_ref, out_ref):
    n = act_ref.shape[1]
    half = n // 2
    maps = maps_ref[...].reshape(n, maps_ref.shape[-1])
    rates = maps[:, 2 * NSTATE :]
    step, decay = rates_of(rates, choice_ref[...], head_ref[...])
    tri = lower(n)
    running = dot(tri, decay, precision=EXACT)
    raw_t = dot(choice_t_ref[...], rates, ((1,), (1,)), precision=EXACT)
    step_t = jax.nn.softplus(raw_t + head_t_ref[:, 0:1])
    decay_t = -jnp.exp(head_t_ref[:, 1:2]) * step_t
    running_t = dot(decay_t, tri, ((1,), (1,)), precision=EXACT)
    b_rows = maps[:, :NSTATE].astype(BF16)
    c_rows = maps[:, NSTATE : 2 * NSTATE].astype(BF16)
    scores = tri * dot(c_rows, b_rows, ((1,), (1,)))
    start = start_ref[0]
    high = start.astype(BF16)
    low = (start - high.astype(F32)).astype(BF16)
    across = dot(c_rows, high) + dot(c_rows, low)
    act = act_ref[0]
    base = wide(jnp.exp(running), spread_ref[...]) * across + skip_ref[...] * act.astype(F32)
    heads = act.shape[1] // HEAD
    first = lax.broadcasted_iota(jnp.int32, (1, 2 * HEAD), 1) < HEAD
    for pair in range(heads // 2):
        cols = slice(2 * HEAD * pair, 2 * HEAD * (pair + 1))
        values = act[:, cols]
        tops, bottoms = [], []
        for h in (2 * pair, 2 * pair + 1):
            row, gain = running_t[h : h + 1], step_t[h : h + 1]
            column = running[:, h : h + 1]
            top = jnp.exp(jnp.minimum(column[:half] - row[:, :half], 0.0)) * scores[:half, :half] * gain[:, :half]
            bottom = jnp.exp(jnp.minimum(column[half:] - row, 0.0)) * scores[half:] * gain
            tops.append(dot(top.astype(BF16), values[:half]))
            bottoms.append(dot(bottom.astype(BF16), values))
        out_ref[:half, cols] = base[:half, cols] + jnp.where(first, tops[0], tops[1])
        out_ref[half:, cols] = base[half:, cols] + jnp.where(first, bottoms[0], bottoms[1])


def finish_body(inside_ref, maps_ref, run_ref, spread_ref, entering_ref, out_ref):
    n = inside_ref.shape[0]
    maps = maps_ref[...].reshape(n, maps_ref.shape[-1])
    c_rows = maps[:, NSTATE : 2 * NSTATE].astype(BF16)
    entering = entering_ref[...]
    high = entering.astype(BF16)
    low = (entering - high.astype(F32)).astype(BF16)
    across = dot(c_rows, high) + dot(c_rows, low)
    out_ref[...] = (inside_ref[...] + wide(jnp.exp(run_ref[...]), spread_ref[...]) * across).astype(BF16)


def scan_output(x, maps, act, dt_bias, decay_log, skip_gain, e):
    subs, rows, cols = act.shape
    tokens = subs * rows
    blocks = tokens // STRETCH
    inner = rows // STRETCH
    heads = cols // HEAD
    n_maps = maps.shape[1]
    lanes = n_maps - 2 * NSTATE
    head = lax.broadcasted_iota(jnp.int32, (lanes, lanes), 0)
    lane = lax.broadcasted_iota(jnp.int32, (lanes, lanes), 1)
    choice = ((head == lane + e * heads) & (lane < heads)).astype(F32)
    choice_t = (
        lax.broadcasted_iota(jnp.int32, (heads, lanes), 1)
        == lax.broadcasted_iota(jnp.int32, (heads, lanes), 0) + e * heads
    ).astype(F32)
    spread = (
        lax.broadcasted_iota(jnp.int32, (lanes, cols), 0)
        == lax.broadcasted_iota(jnp.int32, (lanes, cols), 1) // HEAD
    ).astype(F32)
    per_head = jnp.stack([dt_bias, decay_log])
    head_row = jnp.pad(per_head, ((0, 6), (0, lanes - heads)))
    head_t = jnp.pad(per_head.T, ((0, 0), (0, lanes - 2)))
    skip = jnp.repeat(skip_gain, HEAD)[None, :]
    place = x.reshape(1)

    maps_spec = pl.BlockSpec((STRETCH, n_maps), lambda b, *_: (b, 0))
    act_spec = pl.BlockSpec((1, STRETCH, cols), lambda b, p: ((p[0] + subs - b // inner) % subs, b % inner, 0))
    start_spec = pl.BlockSpec((1, NSTATE, cols), lambda b, *_: (b, 0, 0))
    lane_spec = pl.BlockSpec((STRETCH, lanes), lambda b, *_: (b, 0))
    wide_spec = pl.BlockSpec((STRETCH, cols), lambda b, *_: (b, 0))
    start, runs, final = pl.pallas_call(
        state_body,
        name="states",
        grid_spec=pltpu.PrefetchScalarGridSpec(
            num_scalar_prefetch=1,
            grid=(blocks,),
            in_specs=[maps_spec, act_spec, whole((lanes, lanes)), whole((lanes, cols)), whole((8, lanes))],
            out_specs=[start_spec, lane_spec, whole((NSTATE + 8, cols))],
            scratch_shapes=[pltpu.VMEM((NSTATE, cols), F32), pltpu.VMEM((8, lanes), F32)],
        ),
        out_shape=[
            jax.ShapeDtypeStruct((blocks, NSTATE, cols), F32),
            jax.ShapeDtypeStruct((tokens, lanes), F32),
            jax.ShapeDtypeStruct((NSTATE + 8, cols), F32),
        ],
    )(place, maps, act, choice, spread, head_row)

    gone = [passed_on(final, SPAN, d) for d in range(1, lax.axis_size(SPAN))]

    inside = pl.pallas_call(
        inside_body,
        name="inside",
        grid_spec=pltpu.PrefetchScalarGridSpec(
            num_scalar_prefetch=1,
            grid=(blocks,),
            in_specs=[
                maps_spec,
                act_spec,
                whole((lanes, lanes)),
                whole((heads, lanes)),
                whole((lanes, cols)),
                whole((8, lanes)),
                whole((heads, lanes)),
                whole((1, cols)),
                start_spec,
            ],
            out_specs=wide_spec,
        ),
        out_shape=jax.ShapeDtypeStruct((tokens, cols), F32),
    )(place, maps, act, choice, choice_t, spread, head_row, head_t, skip, start)

    entering = gone[0][:NSTATE]
    decay = gone[0][NSTATE : NSTATE + 1]
    for block in gone[1:]:
        entering = entering + decay * block[:NSTATE]
        decay = decay * block[NSTATE : NSTATE + 1]

    return pl.pallas_call(
        finish_body,
        name="finish",
        grid=(blocks,),
        in_specs=[wide_spec, maps_spec, lane_spec, whole((lanes, cols)), whole((NSTATE, cols))],
        out_specs=wide_spec,
        out_shape=jax.ShapeDtypeStruct((tokens, cols), BF16),
    )(inside, maps, runs, spread, entering)


def shards(
    residual,
    expert_rows,
    expert_ids,
    expert_slots,
    combine_weights,
    norm_gain,
    in_weight,
    conv_weight,
    conv_bias,
    bc_weight,
    dt_weight,
    dt_bias,
    decay_log,
    skip_gain,
):
    own, width = residual.shape
    spans = lax.axis_size(SPAN)
    nx, ny = lax.axis_size("x"), lax.axis_size("y")
    s, e, x, y = (lax.axis_index(axis) for axis in (SPAN, PLANE, "x", "y"))
    local = in_weight.shape[1]
    depth = width // spans

    piece = lax.dynamic_slice_in_dim(in_weight, s * depth, depth, 0)
    maps_weight = jnp.concatenate([bc_weight, dt_weight], axis=1)
    taps = jnp.concatenate([conv_weight, conv_bias[None], jnp.zeros((7 - KCONV, local), F32)], axis=0)
    maps_weights = jnp.stack([maps_weight] + [shifted(maps_weight, "x", -r) for r in range(1, nx)])
    all_taps = jnp.stack([taps] + [shifted(taps, "x", -r) for r in range(1, nx)])
    everyone = lax.all_gather(piece, SPAN + ("x",)).reshape(spans, nx, depth, local)

    returned = lax.all_to_all(expert_rows, PLANE, split_axis=2, concat_axis=1, tiled=True)
    returned, maps_weights, all_taps = lax.optimization_barrier((returned, maps_weights, all_taps))
    capacity = returned.shape[3]
    rows = returned.reshape(returned.shape[1] * capacity, width)
    normed = combine(expert_ids * capacity + expert_slots, combine_weights, rows, residual, norm_gain)

    below = shifted(normed, "y", 1)
    above = shifted(normed, "y", -1)
    above, everyone = lax.optimization_barrier((above, everyone))
    half = own // 2
    far = jnp.concatenate([shifted(below[:half], "y", 1), shifted(above[half:], "y", -1)], axis=0)

    deep = 2
    own_spec = pl.BlockSpec((deep * depth, local), lambda r, k, _: (k, 0))
    other_spec = pl.BlockSpec((deep, 1, depth, local), lambda r, k, p: (k, (p[0] + r + 1) % nx, 0, 0))
    steps = spans // deep

    def projected(units):
        here = project(x, units, in_weight, own_spec, 1, steps)
        return jnp.concatenate([here, project(x, units, everyone, other_spec, nx - 1, steps)], axis=0)

    near_in = projected((normed, above, below))
    far, near_in = lax.optimization_barrier((far, near_in))
    far_in = projected((far,))

    ends = jnp.stack([near_in[:, 0, -8:], near_in[:, 1, -8:], far_in[:, 0, -8:], near_in[:, 2, -8:]], axis=0)
    last = lax.dynamic_index_in_dim(ends, (ny - 1 - y) % ny, 0, keepdims=False)
    rim = passed_on(jnp.roll(last, -1, axis=0), SPAN + ("x",), 1)
    act, part = filter_rows(y, near_in, far_in, rim, all_taps, maps_weights)

    act_here = jnp.stack([act[0]] + [shifted(act[r], "x", r) for r in range(1, nx)])

    part = part.reshape(ny, own, part.shape[1])
    mine = lax.dynamic_index_in_dim(part, y, 0, keepdims=False)
    for d in range(1, ny):
        mine = mine + shifted(lax.dynamic_index_in_dim(part, (y + d) % ny, 0, keepdims=False), "y", d)
    maps = lax.all_gather(mine, PLANE, axis=0, tiled=True)
    return scan_output(x, maps, act_here, dt_bias, decay_log, skip_gain, e)


def solution(mesh):
    spans, plane = mesh.devices.shape
    side = 4
    fine = Mesh(mesh.devices.reshape(spans // 2, 2, plane // side, side), ("z", "c", "x", "y"))
    placed = (
        P(("z", "c", "x", "y"), None),
        P(SPAN, PLANE, None, None, None),
        P(("z", "c", "x", "y"), None),
        P(("z", "c", "x", "y"), None),
        P(("z", "c", "x", "y"), None),
        P(),
        P(None, PLANE),
        P(None, PLANE),
        P(PLANE),
        P(PLANE, None),
        P(PLANE, None),
        P(PLANE),
        P(PLANE),
        P(PLANE),
    )
    return jax.shard_map(shards, mesh=fine, in_specs=placed, out_specs=P(SPAN, PLANE), check_vma=False)
```

```python
import jax
import jax.numpy as jnp
from jax import lax
from jax.experimental import pallas as pl
from jax.experimental.pallas import tpu as pltpu
from jax.sharding import Mesh, PartitionSpec as P

TOPK = 2
KCONV = 4
HEAD = 64
NSTATE = 64
STRETCH = 256
EPS = 1e-06
SPAN = ("z", "c")
PLANE = ("x", "y")
BF16 = jnp.bfloat16
F32 = jnp.float32
EXACT = lax.Precision.HIGHEST


def shifted(value, axis, steps):
    count = lax.axis_size(axis)
    return lax.ppermute(value, axis, [(i, (i + steps) % count) for i in range(count)])


def passed_on(value, axes, steps):
    count = lax.axis_size(axes)
    return lax.ppermute(value, axes, [(i, i + steps) for i in range(count - steps)])


def whole(shape):
    return pl.BlockSpec(shape, lambda *_: (0,) * len(shape))


def dot(a, b, dims=((1,), (0,)), precision=None):
    return lax.dot_general(a, b, (dims, ((), ())), precision=precision, preferred_element_type=F32)


def combine_body(index_ref, weight_ref, rows_ref, residual_ref, gain_ref, out_ref, stream_ref):
    own, width = residual_ref.shape
    slots = rows_ref.shape[0]
    step = 1024
    lane = lax.broadcasted_iota(jnp.int32, (own, slots), 1)
    mix = jnp.zeros((own, slots), F32)
    for k in range(TOPK):
        mix = mix + jnp.where(lane == index_ref[:, k : k + 1], weight_ref[:, k : k + 1], 0.0)
    high = mix.astype(BF16)
    low = (mix - high.astype(F32)).astype(BF16)

    def gather(i, total):
        cols = pl.ds(pl.multiple_of(i * step, step), step)
        rows = rows_ref[:, cols]
        stream = residual_ref[:, cols].astype(F32) + (dot(high, rows) + dot(low, rows))
        stream_ref[:, cols] = stream
        return total + jnp.sum(stream * stream, axis=1, keepdims=True)

    total = lax.fori_loop(0, width // step, gather, jnp.zeros((own, 1), F32))
    factor = lax.rsqrt(total / width + EPS)

    def scale(i, carry):
        cols = pl.ds(pl.multiple_of(i * step, step), step)
        out_ref[:, cols] = (stream_ref[:, cols] * factor * gain_ref[:, cols]).astype(BF16)
        return carry

    lax.fori_loop(0, width // step, scale, 0)


def combine(index, weights, rows, residual, gain):
    own, width = residual.shape
    return pl.pallas_call(
        combine_body,
        name="combine",
        out_shape=jax.ShapeDtypeStruct((own, width), BF16),
        scratch_shapes=[pltpu.VMEM((own, width), F32)],
    )(index, weights, rows, residual, gain.reshape(1, width))


def project_body(*refs):
    _, *x_refs, w_ref, out_ref, acc_ref = refs
    k = pl.program_id(1)
    weight = w_ref[...].reshape(-1, w_ref.shape[-1])
    depth = weight.shape[0]
    rows = x_refs[0].shape[0]
    cols = pl.ds(pl.multiple_of(k * depth, depth), depth)
    left = jnp.concatenate([ref[:, cols] for ref in x_refs], axis=0)
    part = dot(left, weight)

    @pl.when(k == 0)
    def _():
        acc_ref[...] = part

    @pl.when(k > 0)
    def _():
        acc_ref[...] += part

    @pl.when(k == pl.num_programs(1) - 1)
    def _():
        for u in range(len(x_refs)):
            out_ref[0, u] = acc_ref[u * rows : (u + 1) * rows].astype(BF16)


def project(place, units, weight, weight_spec, shards, depth_steps):
    rows, width = units[0].shape
    cols = weight.shape[-1]
    return pl.pallas_call(
        project_body,
        name="project",
        grid_spec=pltpu.PrefetchScalarGridSpec(
            num_scalar_prefetch=1,
            grid=(shards, depth_steps),
            in_specs=[whole((rows, width)) for _ in units] + [weight_spec],
            out_specs=pl.BlockSpec((1, len(units), rows, cols), lambda r, k, _: (r, 0, 0, 0)),
            scratch_shapes=[pltpu.VMEM((len(units) * rows, cols), F32)],
        ),
        out_shape=jax.ShapeDtypeStruct((shards, len(units), rows, cols), BF16),
    )(place.reshape(1), *units, weight)


def filter_body(place_ref, near_ref, far_ref, rim_ref, taps_ref, weight_ref, act_ref, part_ref, pad_ref):
    r = pl.program_id(0)
    near, rows, cols = near_ref.shape[1:]
    y = place_ref[0]
    order = (0, 1, 3)
    units = near + 1
    pad_ref[0:8] = rim_ref[0].astype(F32)
    for u in range(near):
        at = (y + order[u]) % units
        pad_ref[pl.ds(pl.multiple_of(8 + at * rows, 8), rows)] = near_ref[0, u].astype(F32)
    at = (y + 2) % units
    pad_ref[pl.ds(pl.multiple_of(8 + at * rows, 8), rows)] = far_ref[0, 0].astype(F32)
    total = units * rows
    step = 128
    for i in range(total // step):
        filtered = taps_ref[0, KCONV : KCONV + 1, :]
        for tap in range(KCONV):
            first = 8 - (KCONV - 1) + tap + i * step
            filtered = filtered + taps_ref[0, tap : tap + 1, :] * pad_ref[first : first + step]
        act_ref[0, i * step : (i + 1) * step] = jax.nn.silu(filtered).astype(BF16)
    part = dot(act_ref[0], weight_ref[0])

    @pl.when(r == 0)
    def _():
        part_ref[...] = part

    @pl.when(r > 0)
    def _():
        part_ref[...] += part


def filter_rows(y, near, far, rim, taps, weights):
    shards, n_near, rows, cols = near.shape
    total = (n_near + 1) * rows
    maps = weights.shape[-1]
    return pl.pallas_call(
        filter_body,
        name="filter",
        grid_spec=pltpu.PrefetchScalarGridSpec(
            num_scalar_prefetch=1,
            grid=(shards,),
            in_specs=[
                pl.BlockSpec((1, n_near, rows, cols), lambda r, _: (r, 0, 0, 0)),
                pl.BlockSpec((1, 1, rows, cols), lambda r, _: (r, 0, 0, 0)),
                pl.BlockSpec((1, 8, cols), lambda r, _: (r, 0, 0)),
                pl.BlockSpec((1, 8, cols), lambda r, _: (r, 0, 0)),
                pl.BlockSpec((1, cols, maps), lambda r, _: (r, 0, 0)),
            ],
            out_specs=[
                pl.BlockSpec((1, total, cols), lambda r, _: (r, 0, 0)),
                pl.BlockSpec((total, maps), lambda r, _: (0, 0)),
            ],
            scratch_shapes=[pltpu.VMEM((total + 8, cols), F32)],
        ),
        out_shape=[
            jax.ShapeDtypeStruct((shards, total, cols), BF16),
            jax.ShapeDtypeStruct((total, maps), F32),
        ],
    )(y.reshape(1), near, far, rim, taps, weights)


def wide(narrow, spread):
    return dot(narrow, spread, precision=EXACT)


def rates_of(rate_rows, choice, head_row):
    raw = wide(rate_rows, choice)
    step = jax.nn.softplus(raw + head_row[0:1])
    return step, -jnp.exp(head_row[1:2]) * step


def lower(n):
    return (
        lax.broadcasted_iota(jnp.int32, (n, n), 0) >= lax.broadcasted_iota(jnp.int32, (n, n), 1)
    ).astype(F32)


def state_body(place_ref, maps_ref, act_ref, choice_ref, spread_ref, head_ref, start_ref, run_ref, final_ref, state_ref, sum_ref):
    b = pl.program_id(0)
    n = act_ref.shape[1]

    @pl.when(b == 0)
    def _():
        state_ref[...] = jnp.zeros_like(state_ref)
        sum_ref[...] = jnp.zeros_like(sum_ref)

    maps = maps_ref[...].reshape(n, maps_ref.shape[-1])
    step, decay = rates_of(maps[:, 2 * NSTATE :], choice_ref[...], head_ref[...])
    running = dot(lower(n), decay, precision=EXACT)
    total = running[n - 1 : n]
    spread = spread_ref[...]
    carried = wide(jnp.exp(total - running) * step, spread) * act_ref[0].astype(F32)
    high = carried.astype(BF16)
    low = (carried - high.astype(F32)).astype(BF16)
    b_rows = maps[:, :NSTATE].astype(BF16)
    state = dot(b_rows, high, ((0,), (0,))) + dot(b_rows, low, ((0,), (0,)))
    run_ref[...] = sum_ref[0:1] + running
    start_ref[0] = state_ref[...]
    state_ref[...] = wide(jnp.broadcast_to(jnp.exp(total), (8, total.shape[1])), spread)[0:1] * state_ref[...] + state
    sum_ref[...] = sum_ref[...] + total

    @pl.when(b == pl.num_programs(0) - 1)
    def _():
        final_ref[0:NSTATE] = state_ref[...]
        final_ref[NSTATE : NSTATE + 8] = wide(jnp.exp(sum_ref[...]), spread)


def inside_body(place_ref, maps_ref, act_ref, choice_ref, choice_t_ref, spread_ref, head_ref, head_t_ref, skip_ref, start_ref, out_ref):
    n = act_ref.shape[1]
    half = n // 2
    maps = maps_ref[...].reshape(n, maps_ref.shape[-1])
    rates = maps[:, 2 * NSTATE :]
    step, decay = rates_of(rates, choice_ref[...], head_ref[...])
    tri = lower(n)
    running = dot(tri, decay, precision=EXACT)
    raw_t = dot(choice_t_ref[...], rates, ((1,), (1,)), precision=EXACT)
    step_t = jax.nn.softplus(raw_t + head_t_ref[:, 0:1])
    decay_t = -jnp.exp(head_t_ref[:, 1:2]) * step_t
    running_t = dot(decay_t, tri, ((1,), (1,)), precision=EXACT)
    b_rows = maps[:, :NSTATE].astype(BF16)
    c_rows = maps[:, NSTATE : 2 * NSTATE].astype(BF16)
    scores = tri * dot(c_rows, b_rows, ((1,), (1,)))
    start = start_ref[0]
    high = start.astype(BF16)
    low = (start - high.astype(F32)).astype(BF16)
    across = dot(c_rows, high) + dot(c_rows, low)
    act = act_ref[0]
    base = wide(jnp.exp(running), spread_ref[...]) * across + skip_ref[...] * act.astype(F32)
    heads = act.shape[1] // HEAD
    first = lax.broadcasted_iota(jnp.int32, (1, 2 * HEAD), 1) < HEAD
    for pair in range(heads // 2):
        cols = slice(2 * HEAD * pair, 2 * HEAD * (pair + 1))
        values = act[:, cols]
        tops, bottoms = [], []
        for h in (2 * pair, 2 * pair + 1):
            row, gain = running_t[h : h + 1], step_t[h : h + 1]
            column = running[:, h : h + 1]
            top = jnp.exp(jnp.minimum(column[:half] - row[:, :half], 0.0)) * scores[:half, :half] * gain[:, :half]
            bottom = jnp.exp(jnp.minimum(column[half:] - row, 0.0)) * scores[half:] * gain
            tops.append(dot(top.astype(BF16), values[:half]))
            bottoms.append(dot(bottom.astype(BF16), values))
        out_ref[:half, cols] = base[:half, cols] + jnp.where(first, tops[0], tops[1])
        out_ref[half:, cols] = base[half:, cols] + jnp.where(first, bottoms[0], bottoms[1])


def finish_body(inside_ref, maps_ref, run_ref, spread_ref, entering_ref, out_ref):
    n = inside_ref.shape[0]
    maps = maps_ref[...].reshape(n, maps_ref.shape[-1])
    c_rows = maps[:, NSTATE : 2 * NSTATE].astype(BF16)
    entering = entering_ref[...]
    high = entering.astype(BF16)
    low = (entering - high.astype(F32)).astype(BF16)
    across = dot(c_rows, high) + dot(c_rows, low)
    out_ref[...] = (inside_ref[...] + wide(jnp.exp(run_ref[...]), spread_ref[...]) * across).astype(BF16)


def scan_output(x, maps, act, dt_bias, decay_log, skip_gain, e):
    subs, rows, cols = act.shape
    tokens = subs * rows
    blocks = tokens // STRETCH
    inner = rows // STRETCH
    heads = cols // HEAD
    n_maps = maps.shape[1]
    lanes = n_maps - 2 * NSTATE
    head = lax.broadcasted_iota(jnp.int32, (lanes, lanes), 0)
    lane = lax.broadcasted_iota(jnp.int32, (lanes, lanes), 1)
    choice = ((head == lane + e * heads) & (lane < heads)).astype(F32)
    choice_t = (
        lax.broadcasted_iota(jnp.int32, (heads, lanes), 1)
        == lax.broadcasted_iota(jnp.int32, (heads, lanes), 0) + e * heads
    ).astype(F32)
    spread = (
        lax.broadcasted_iota(jnp.int32, (lanes, cols), 0)
        == lax.broadcasted_iota(jnp.int32, (lanes, cols), 1) // HEAD
    ).astype(F32)
    per_head = jnp.stack([dt_bias, decay_log])
    head_row = jnp.pad(per_head, ((0, 6), (0, lanes - heads)))
    head_t = jnp.pad(per_head.T, ((0, 0), (0, lanes - 2)))
    skip = jnp.repeat(skip_gain, HEAD)[None, :]
    place = x.reshape(1)

    maps_spec = pl.BlockSpec((STRETCH, n_maps), lambda b, *_: (b, 0))
    act_spec = pl.BlockSpec((1, STRETCH, cols), lambda b, p: ((p[0] + subs - b // inner) % subs, b % inner, 0))
    start_spec = pl.BlockSpec((1, NSTATE, cols), lambda b, *_: (b, 0, 0))
    lane_spec = pl.BlockSpec((STRETCH, lanes), lambda b, *_: (b, 0))
    wide_spec = pl.BlockSpec((STRETCH, cols), lambda b, *_: (b, 0))
    start, runs, final = pl.pallas_call(
        state_body,
        name="states",
        grid_spec=pltpu.PrefetchScalarGridSpec(
            num_scalar_prefetch=1,
            grid=(blocks,),
            in_specs=[maps_spec, act_spec, whole((lanes, lanes)), whole((lanes, cols)), whole((8, lanes))],
            out_specs=[start_spec, lane_spec, whole((NSTATE + 8, cols))],
            scratch_shapes=[pltpu.VMEM((NSTATE, cols), F32), pltpu.VMEM((8, lanes), F32)],
        ),
        out_shape=[
            jax.ShapeDtypeStruct((blocks, NSTATE, cols), F32),
            jax.ShapeDtypeStruct((tokens, lanes), F32),
            jax.ShapeDtypeStruct((NSTATE + 8, cols), F32),
        ],
    )(place, maps, act, choice, spread, head_row)

    gone = [passed_on(final, SPAN, d) for d in range(1, lax.axis_size(SPAN))]

    inside = pl.pallas_call(
        inside_body,
        name="inside",
        grid_spec=pltpu.PrefetchScalarGridSpec(
            num_scalar_prefetch=1,
            grid=(blocks,),
            in_specs=[
                maps_spec,
                act_spec,
                whole((lanes, lanes)),
                whole((heads, lanes)),
                whole((lanes, cols)),
                whole((8, lanes)),
                whole((heads, lanes)),
                whole((1, cols)),
                start_spec,
            ],
            out_specs=wide_spec,
        ),
        out_shape=jax.ShapeDtypeStruct((tokens, cols), F32),
    )(place, maps, act, choice, choice_t, spread, head_row, head_t, skip, start)

    entering = gone[0][:NSTATE]
    decay = gone[0][NSTATE : NSTATE + 1]
    for block in gone[1:]:
        entering = entering + decay * block[:NSTATE]
        decay = decay * block[NSTATE : NSTATE + 1]

    return pl.pallas_call(
        finish_body,
        name="finish",
        grid=(blocks,),
        in_specs=[wide_spec, maps_spec, lane_spec, whole((lanes, cols)), whole((NSTATE, cols))],
        out_specs=wide_spec,
        out_shape=jax.ShapeDtypeStruct((tokens, cols), BF16),
    )(inside, maps, runs, spread, entering)


def shards(
    residual,
    expert_rows,
    expert_ids,
    expert_slots,
    combine_weights,
    norm_gain,
    in_weight,
    conv_weight,
    conv_bias,
    bc_weight,
    dt_weight,
    dt_bias,
    decay_log,
    skip_gain,
):
    own, width = residual.shape
    spans = lax.axis_size(SPAN)
    nx, ny = lax.axis_size("x"), lax.axis_size("y")
    s, e, x, y = (lax.axis_index(axis) for axis in (SPAN, PLANE, "x", "y"))
    local = in_weight.shape[1]
    depth = width // spans

    piece = lax.dynamic_slice_in_dim(in_weight, s * depth, depth, 0)
    maps_weight = jnp.concatenate([bc_weight, dt_weight], axis=1)
    taps = jnp.concatenate([conv_weight, conv_bias[None], jnp.zeros((7 - KCONV, local), F32)], axis=0)
    everyone = lax.all_gather(piece, SPAN + ("x",)).reshape(spans, nx, depth, local)

    returned = lax.all_to_all(expert_rows, PLANE, split_axis=2, concat_axis=1, tiled=True)
    capacity = returned.shape[3]
    rows = returned.reshape(returned.shape[1] * capacity, width)
    normed = combine(expert_ids * capacity + expert_slots, combine_weights, rows, residual, norm_gain)

    below = shifted(normed, "y", 1)
    above = shifted(normed, "y", -1)
    maps_weight, taps, _ = lax.optimization_barrier((maps_weight, taps, normed))
    maps_weights = jnp.stack([maps_weight] + [shifted(maps_weight, "x", -r) for r in range(1, nx)])
    all_taps = jnp.stack([taps] + [shifted(taps, "x", -r) for r in range(1, nx)])
    above, everyone, maps_weights, all_taps = lax.optimization_barrier((above, everyone, maps_weights, all_taps))
    half = own // 2
    far = jnp.concatenate([shifted(below[:half], "y", 1), shifted(above[half:], "y", -1)], axis=0)

    deep = 2
    own_spec = pl.BlockSpec((deep * depth, local), lambda r, k, _: (k, 0))
    other_spec = pl.BlockSpec((deep, 1, depth, local), lambda r, k, p: (k, (p[0] + r + 1) % nx, 0, 0))
    steps = spans // deep

    def projected(units):
        here = project(x, units, in_weight, own_spec, 1, steps)
        return jnp.concatenate([here, project(x, units, everyone, other_spec, nx - 1, steps)], axis=0)

    near_in = projected((normed, above, below))
    far, near_in = lax.optimization_barrier((far, near_in))
    far_in = projected((far,))

    ends = jnp.stack([near_in[:, 0, -8:], near_in[:, 1, -8:], far_in[:, 0, -8:], near_in[:, 2, -8:]], axis=0)
    last = lax.dynamic_index_in_dim(ends, (ny - 1 - y) % ny, 0, keepdims=False)
    rim = passed_on(jnp.roll(last, -1, axis=0), SPAN + ("x",), 1)
    act, part = filter_rows(y, near_in, far_in, rim, all_taps, maps_weights)

    act_here = jnp.stack([act[0]] + [shifted(act[r], "x", r) for r in range(1, nx)])

    part = part.reshape(ny, own, part.shape[1])
    mine = lax.dynamic_index_in_dim(part, y, 0, keepdims=False)
    for d in range(1, ny):
        mine = mine + shifted(lax.dynamic_index_in_dim(part, (y + d) % ny, 0, keepdims=False), "y", d)
    maps = lax.all_gather(mine, PLANE, axis=0, tiled=True)
    return scan_output(x, maps, act_here, dt_bias, decay_log, skip_gain, e)


def solution(mesh):
    spans, plane = mesh.devices.shape
    side = 4
    fine = Mesh(mesh.devices.reshape(spans // 2, 2, plane // side, side), ("z", "c", "x", "y"))
    placed = (
        P(("z", "c", "x", "y"), None),
        P(SPAN, PLANE, None, None, None),
        P(("z", "c", "x", "y"), None),
        P(("z", "c", "x", "y"), None),
        P(("z", "c", "x", "y"), None),
        P(),
        P(None, PLANE),
        P(None, PLANE),
        P(PLANE),
        P(PLANE, None),
        P(PLANE, None),
        P(PLANE),
        P(PLANE),
        P(PLANE),
    )
    return jax.shard_map(shards, mesh=fine, in_specs=placed, out_specs=P(SPAN, PLANE), check_vma=False)
```

```python
import jax
import jax.numpy as jnp
from jax import lax
from jax.experimental import pallas as pl
from jax.experimental.pallas import tpu as pltpu
from jax.sharding import Mesh, PartitionSpec as P

TOPK = 2
KCONV = 4
HEAD = 64
NSTATE = 64
STRETCH = 256
EPS = 1e-06
SPAN = ("z", "c")
PLANE = ("x", "y")
BF16 = jnp.bfloat16
F32 = jnp.float32
EXACT = lax.Precision.HIGHEST


def shifted(value, axis, steps):
    count = lax.axis_size(axis)
    return lax.ppermute(value, axis, [(i, (i + steps) % count) for i in range(count)])


def passed_on(value, axes, steps):
    count = lax.axis_size(axes)
    return lax.ppermute(value, axes, [(i, i + steps) for i in range(count - steps)])


def whole(shape):
    return pl.BlockSpec(shape, lambda *_: (0,) * len(shape))


def dot(a, b, dims=((1,), (0,)), precision=None):
    return lax.dot_general(a, b, (dims, ((), ())), precision=precision, preferred_element_type=F32)


def combine_body(index_ref, weight_ref, rows_ref, residual_ref, gain_ref, out_ref, stream_ref):
    own, width = residual_ref.shape
    slots = rows_ref.shape[0]
    step = 1024
    lane = lax.broadcasted_iota(jnp.int32, (own, slots), 1)
    mix = jnp.zeros((own, slots), F32)
    for k in range(TOPK):
        mix = mix + jnp.where(lane == index_ref[:, k : k + 1], weight_ref[:, k : k + 1], 0.0)
    high = mix.astype(BF16)
    low = (mix - high.astype(F32)).astype(BF16)

    def gather(i, total):
        cols = pl.ds(pl.multiple_of(i * step, step), step)
        rows = rows_ref[:, cols]
        stream = residual_ref[:, cols].astype(F32) + (dot(high, rows) + dot(low, rows))
        stream_ref[:, cols] = stream
        return total + jnp.sum(stream * stream, axis=1, keepdims=True)

    total = lax.fori_loop(0, width // step, gather, jnp.zeros((own, 1), F32))
    factor = lax.rsqrt(total / width + EPS)

    def scale(i, carry):
        cols = pl.ds(pl.multiple_of(i * step, step), step)
        out_ref[:, cols] = (stream_ref[:, cols] * factor * gain_ref[:, cols]).astype(BF16)
        return carry

    lax.fori_loop(0, width // step, scale, 0)


def combine(index, weights, rows, residual, gain):
    own, width = residual.shape
    return pl.pallas_call(
        combine_body,
        name="combine",
        out_shape=jax.ShapeDtypeStruct((own, width), BF16),
        scratch_shapes=[pltpu.VMEM((own, width), F32)],
    )(index, weights, rows, residual, gain.reshape(1, width))


def project_body(*refs):
    _, *x_refs, w_ref, out_ref, acc_ref = refs
    k = pl.program_id(1)
    weight = w_ref[...].reshape(-1, w_ref.shape[-1])
    depth = weight.shape[0]
    rows = x_refs[0].shape[0]
    cols = pl.ds(pl.multiple_of(k * depth, depth), depth)
    left = jnp.concatenate([ref[:, cols] for ref in x_refs], axis=0)
    part = dot(left, weight)

    @pl.when(k == 0)
    def _():
        acc_ref[...] = part

    @pl.when(k > 0)
    def _():
        acc_ref[...] += part

    @pl.when(k == pl.num_programs(1) - 1)
    def _():
        for u in range(len(x_refs)):
            out_ref[0, u] = acc_ref[u * rows : (u + 1) * rows].astype(BF16)


def project(place, units, weight, weight_spec, shards, depth_steps):
    rows, width = units[0].shape
    cols = weight.shape[-1]
    return pl.pallas_call(
        project_body,
        name="project",
        grid_spec=pltpu.PrefetchScalarGridSpec(
            num_scalar_prefetch=1,
            grid=(shards, depth_steps),
            in_specs=[whole((rows, width)) for _ in units] + [weight_spec],
            out_specs=pl.BlockSpec((1, len(units), rows, cols), lambda r, k, _: (r, 0, 0, 0)),
            scratch_shapes=[pltpu.VMEM((len(units) * rows, cols), F32)],
        ),
        out_shape=jax.ShapeDtypeStruct((shards, len(units), rows, cols), BF16),
    )(place.reshape(1), *units, weight)


def filter_body(place_ref, near_ref, far_ref, rim_ref, taps_ref, weight_ref, act_ref, part_ref, pad_ref):
    r = pl.program_id(0)
    near, rows, cols = near_ref.shape[1:]
    y = place_ref[0]
    order = (0, 1, 3)
    units = near + 1
    pad_ref[0:8] = rim_ref[0].astype(F32)
    for u in range(near):
        at = (y + order[u]) % units
        pad_ref[pl.ds(pl.multiple_of(8 + at * rows, 8), rows)] = near_ref[0, u].astype(F32)
    at = (y + 2) % units
    pad_ref[pl.ds(pl.multiple_of(8 + at * rows, 8), rows)] = far_ref[0, 0].astype(F32)
    total = units * rows
    step = 128
    for i in range(total // step):
        filtered = taps_ref[0, KCONV : KCONV + 1, :]
        for tap in range(KCONV):
            first = 8 - (KCONV - 1) + tap + i * step
            filtered = filtered + taps_ref[0, tap : tap + 1, :] * pad_ref[first : first + step]
        act_ref[0, i * step : (i + 1) * step] = jax.nn.silu(filtered).astype(BF16)
    part = dot(act_ref[0], weight_ref[0])

    @pl.when(r == 0)
    def _():
        part_ref[...] = part

    @pl.when(r > 0)
    def _():
        part_ref[...] += part


def filter_rows(y, near, far, rim, taps, weights):
    shards, n_near, rows, cols = near.shape
    total = (n_near + 1) * rows
    maps = weights.shape[-1]
    return pl.pallas_call(
        filter_body,
        name="filter",
        grid_spec=pltpu.PrefetchScalarGridSpec(
            num_scalar_prefetch=1,
            grid=(shards,),
            in_specs=[
                pl.BlockSpec((1, n_near, rows, cols), lambda r, _: (r, 0, 0, 0)),
                pl.BlockSpec((1, 1, rows, cols), lambda r, _: (r, 0, 0, 0)),
                pl.BlockSpec((1, 8, cols), lambda r, _: (r, 0, 0)),
                pl.BlockSpec((1, 8, cols), lambda r, _: (r, 0, 0)),
                pl.BlockSpec((1, cols, maps), lambda r, _: (r, 0, 0)),
            ],
            out_specs=[
                pl.BlockSpec((1, total, cols), lambda r, _: (r, 0, 0)),
                pl.BlockSpec((total, maps), lambda r, _: (0, 0)),
            ],
            scratch_shapes=[pltpu.VMEM((total + 8, cols), F32)],
        ),
        out_shape=[
            jax.ShapeDtypeStruct((shards, total, cols), BF16),
            jax.ShapeDtypeStruct((total, maps), F32),
        ],
    )(y.reshape(1), near, far, rim, taps, weights)


def wide(narrow, spread):
    return dot(narrow, spread, precision=EXACT)


def rates_of(rate_rows, choice, head_row):
    raw = wide(rate_rows, choice)
    step = jax.nn.softplus(raw + head_row[0:1])
    return step, -jnp.exp(head_row[1:2]) * step


def lower(n):
    return (
        lax.broadcasted_iota(jnp.int32, (n, n), 0) >= lax.broadcasted_iota(jnp.int32, (n, n), 1)
    ).astype(F32)


def state_body(place_ref, maps_ref, act_ref, choice_ref, spread_ref, head_ref, start_ref, run_ref, final_ref, state_ref, sum_ref):
    b = pl.program_id(0)
    n = act_ref.shape[1]

    @pl.when(b == 0)
    def _():
        state_ref[...] = jnp.zeros_like(state_ref)
        sum_ref[...] = jnp.zeros_like(sum_ref)

    maps = maps_ref[...].reshape(n, maps_ref.shape[-1])
    step, decay = rates_of(maps[:, 2 * NSTATE :], choice_ref[...], head_ref[...])
    running = dot(lower(n), decay, precision=EXACT)
    total = running[n - 1 : n]
    spread = spread_ref[...]
    carried = wide(jnp.exp(total - running) * step, spread) * act_ref[0].astype(F32)
    high = carried.astype(BF16)
    low = (carried - high.astype(F32)).astype(BF16)
    b_rows = maps[:, :NSTATE].astype(BF16)
    state = dot(b_rows, high, ((0,), (0,))) + dot(b_rows, low, ((0,), (0,)))
    run_ref[...] = sum_ref[0:1] + running
    start_ref[0] = state_ref[...]
    state_ref[...] = wide(jnp.broadcast_to(jnp.exp(total), (8, total.shape[1])), spread)[0:1] * state_ref[...] + state
    sum_ref[...] = sum_ref[...] + total

    @pl.when(b == pl.num_programs(0) - 1)
    def _():
        final_ref[0:NSTATE] = state_ref[...]
        final_ref[NSTATE : NSTATE + 8] = wide(jnp.exp(sum_ref[...]), spread)


def inside_body(place_ref, maps_ref, act_ref, choice_ref, choice_t_ref, spread_ref, head_ref, head_t_ref, skip_ref, start_ref, out_ref):
    n = act_ref.shape[1]
    half = n // 2
    maps = maps_ref[...].reshape(n, maps_ref.shape[-1])
    rates = maps[:, 2 * NSTATE :]
    step, decay = rates_of(rates, choice_ref[...], head_ref[...])
    tri = lower(n)
    running = dot(tri, decay, precision=EXACT)
    raw_t = dot(choice_t_ref[...], rates, ((1,), (1,)), precision=EXACT)
    step_t = jax.nn.softplus(raw_t + head_t_ref[:, 0:1])
    decay_t = -jnp.exp(head_t_ref[:, 1:2]) * step_t
    running_t = dot(decay_t, tri, ((1,), (1,)), precision=EXACT)
    b_rows = maps[:, :NSTATE].astype(BF16)
    c_rows = maps[:, NSTATE : 2 * NSTATE].astype(BF16)
    scores = tri * dot(c_rows, b_rows, ((1,), (1,)))
    start = start_ref[0]
    high = start.astype(BF16)
    low = (start - high.astype(F32)).astype(BF16)
    across = dot(c_rows, high) + dot(c_rows, low)
    act = act_ref[0]
    base = wide(jnp.exp(running), spread_ref[...]) * across + skip_ref[...] * act.astype(F32)
    heads = act.shape[1] // HEAD
    first = lax.broadcasted_iota(jnp.int32, (1, 2 * HEAD), 1) < HEAD
    for pair in range(heads // 2):
        cols = slice(2 * HEAD * pair, 2 * HEAD * (pair + 1))
        values = act[:, cols]
        tops, bottoms = [], []
        for h in (2 * pair, 2 * pair + 1):
            row, gain = running_t[h : h + 1], step_t[h : h + 1]
            column = running[:, h : h + 1]
            top = jnp.exp(jnp.minimum(column[:half] - row[:, :half], 0.0)) * scores[:half, :half] * gain[:, :half]
            bottom = jnp.exp(jnp.minimum(column[half:] - row, 0.0)) * scores[half:] * gain
            tops.append(dot(top.astype(BF16), values[:half]))
            bottoms.append(dot(bottom.astype(BF16), values))
        out_ref[:half, cols] = base[:half, cols] + jnp.where(first, tops[0], tops[1])
        out_ref[half:, cols] = base[half:, cols] + jnp.where(first, bottoms[0], bottoms[1])


def finish_body(inside_ref, maps_ref, run_ref, spread_ref, entering_ref, out_ref):
    n = inside_ref.shape[0]
    maps = maps_ref[...].reshape(n, maps_ref.shape[-1])
    c_rows = maps[:, NSTATE : 2 * NSTATE].astype(BF16)
    entering = entering_ref[...]
    high = entering.astype(BF16)
    low = (entering - high.astype(F32)).astype(BF16)
    across = dot(c_rows, high) + dot(c_rows, low)
    out_ref[...] = (inside_ref[...] + wide(jnp.exp(run_ref[...]), spread_ref[...]) * across).astype(BF16)


def scan_output(x, maps, act, dt_bias, decay_log, skip_gain, e):
    subs, rows, cols = act.shape
    tokens = subs * rows
    blocks = tokens // STRETCH
    inner = rows // STRETCH
    heads = cols // HEAD
    n_maps = maps.shape[1]
    lanes = n_maps - 2 * NSTATE
    head = lax.broadcasted_iota(jnp.int32, (lanes, lanes), 0)
    lane = lax.broadcasted_iota(jnp.int32, (lanes, lanes), 1)
    choice = ((head == lane + e * heads) & (lane < heads)).astype(F32)
    choice_t = (
        lax.broadcasted_iota(jnp.int32, (heads, lanes), 1)
        == lax.broadcasted_iota(jnp.int32, (heads, lanes), 0) + e * heads
    ).astype(F32)
    spread = (
        lax.broadcasted_iota(jnp.int32, (lanes, cols), 0)
        == lax.broadcasted_iota(jnp.int32, (lanes, cols), 1) // HEAD
    ).astype(F32)
    per_head = jnp.stack([dt_bias, decay_log])
    head_row = jnp.pad(per_head, ((0, 6), (0, lanes - heads)))
    head_t = jnp.pad(per_head.T, ((0, 0), (0, lanes - 2)))
    skip = jnp.repeat(skip_gain, HEAD)[None, :]
    place = x.reshape(1)

    maps_spec = pl.BlockSpec((STRETCH, n_maps), lambda b, *_: (b, 0))
    act_spec = pl.BlockSpec((1, STRETCH, cols), lambda b, p: ((p[0] + subs - b // inner) % subs, b % inner, 0))
    start_spec = pl.BlockSpec((1, NSTATE, cols), lambda b, *_: (b, 0, 0))
    lane_spec = pl.BlockSpec((STRETCH, lanes), lambda b, *_: (b, 0))
    wide_spec = pl.BlockSpec((STRETCH, cols), lambda b, *_: (b, 0))
    start, runs, final = pl.pallas_call(
        state_body,
        name="states",
        grid_spec=pltpu.PrefetchScalarGridSpec(
            num_scalar_prefetch=1,
            grid=(blocks,),
            in_specs=[maps_spec, act_spec, whole((lanes, lanes)), whole((lanes, cols)), whole((8, lanes))],
            out_specs=[start_spec, lane_spec, whole((NSTATE + 8, cols))],
            scratch_shapes=[pltpu.VMEM((NSTATE, cols), F32), pltpu.VMEM((8, lanes), F32)],
        ),
        out_shape=[
            jax.ShapeDtypeStruct((blocks, NSTATE, cols), F32),
            jax.ShapeDtypeStruct((tokens, lanes), F32),
            jax.ShapeDtypeStruct((NSTATE + 8, cols), F32),
        ],
    )(place, maps, act, choice, spread, head_row)

    gone = [passed_on(final, SPAN, d) for d in range(1, lax.axis_size(SPAN))]

    inside = pl.pallas_call(
        inside_body,
        name="inside",
        grid_spec=pltpu.PrefetchScalarGridSpec(
            num_scalar_prefetch=1,
            grid=(blocks,),
            in_specs=[
                maps_spec,
                act_spec,
                whole((lanes, lanes)),
                whole((heads, lanes)),
                whole((lanes, cols)),
                whole((8, lanes)),
                whole((heads, lanes)),
                whole((1, cols)),
                start_spec,
            ],
            out_specs=wide_spec,
        ),
        out_shape=jax.ShapeDtypeStruct((tokens, cols), F32),
    )(place, maps, act, choice, choice_t, spread, head_row, head_t, skip, start)

    entering = gone[0][:NSTATE]
    decay = gone[0][NSTATE : NSTATE + 1]
    for block in gone[1:]:
        entering = entering + decay * block[:NSTATE]
        decay = decay * block[NSTATE : NSTATE + 1]

    return pl.pallas_call(
        finish_body,
        name="finish",
        grid=(blocks,),
        in_specs=[wide_spec, maps_spec, lane_spec, whole((lanes, cols)), whole((NSTATE, cols))],
        out_specs=wide_spec,
        out_shape=jax.ShapeDtypeStruct((tokens, cols), BF16),
    )(inside, maps, runs, spread, entering)


def shards(
    residual,
    expert_rows,
    expert_ids,
    expert_slots,
    combine_weights,
    norm_gain,
    in_weight,
    conv_weight,
    conv_bias,
    bc_weight,
    dt_weight,
    dt_bias,
    decay_log,
    skip_gain,
):
    own, width = residual.shape
    spans = lax.axis_size(SPAN)
    nx, ny = lax.axis_size("x"), lax.axis_size("y")
    s, e, x, y = (lax.axis_index(axis) for axis in (SPAN, PLANE, "x", "y"))
    local = in_weight.shape[1]
    depth = width // spans

    piece = lax.dynamic_slice_in_dim(in_weight, s * depth, depth, 0)
    maps_weight = jnp.concatenate([bc_weight, dt_weight], axis=1)
    taps = jnp.concatenate([conv_weight, conv_bias[None], jnp.zeros((7 - KCONV, local), F32)], axis=0)
    everyone = lax.all_gather(piece, SPAN + ("x",)).reshape(spans, nx, depth, local)

    returned = lax.all_to_all(expert_rows, PLANE, split_axis=2, concat_axis=1, tiled=True)
    capacity = returned.shape[3]
    rows = returned.reshape(returned.shape[1] * capacity, width)
    normed = combine(expert_ids * capacity + expert_slots, combine_weights, rows, residual, norm_gain)

    below = shifted(normed, "y", 1)
    above = shifted(normed, "y", -1)
    maps_weight, taps, _ = lax.optimization_barrier((maps_weight, taps, normed))
    maps_weights = jnp.stack([maps_weight] + [shifted(maps_weight, "x", -r) for r in range(1, nx)])
    all_taps = jnp.stack([taps] + [shifted(taps, "x", -r) for r in range(1, nx)])
    above, everyone, maps_weights, all_taps = lax.optimization_barrier((above, everyone, maps_weights, all_taps))
    half = own // 2
    far = jnp.concatenate([shifted(below[:half], "y", 1), shifted(above[half:], "y", -1)], axis=0)

    deep = 4
    own_spec = pl.BlockSpec((deep * depth, local), lambda r, k, _: (k, 0))
    other_spec = pl.BlockSpec((deep, 1, depth, local), lambda r, k, p: (k, (p[0] + r + 1) % nx, 0, 0))
    steps = spans // deep

    def projected(units):
        here = project(x, units, in_weight, own_spec, 1, steps)
        return jnp.concatenate([here, project(x, units, everyone, other_spec, nx - 1, steps)], axis=0)

    near_in = projected((normed, above, below))
    far, near_in = lax.optimization_barrier((far, near_in))
    far_in = projected((far,))

    ends = jnp.stack([near_in[:, 0, -8:], near_in[:, 1, -8:], far_in[:, 0, -8:], near_in[:, 2, -8:]], axis=0)
    last = lax.dynamic_index_in_dim(ends, (ny - 1 - y) % ny, 0, keepdims=False)
    rim = passed_on(jnp.roll(last, -1, axis=0), SPAN + ("x",), 1)
    act, part = filter_rows(y, near_in, far_in, rim, all_taps, maps_weights)

    act_here = jnp.stack([act[0]] + [shifted(act[r], "x", r) for r in range(1, nx)])

    part = part.reshape(ny, own, part.shape[1])
    mine = lax.dynamic_index_in_dim(part, y, 0, keepdims=False)
    for d in range(1, ny):
        mine = mine + shifted(lax.dynamic_index_in_dim(part, (y + d) % ny, 0, keepdims=False), "y", d)
    maps = lax.all_gather(mine, PLANE, axis=0, tiled=True)
    return scan_output(x, maps, act_here, dt_bias, decay_log, skip_gain, e)


def solution(mesh):
    spans, plane = mesh.devices.shape
    side = 4
    fine = Mesh(mesh.devices.reshape(spans // 2, 2, plane // side, side), ("z", "c", "x", "y"))
    placed = (
        P(("z", "c", "x", "y"), None),
        P(SPAN, PLANE, None, None, None),
        P(("z", "c", "x", "y"), None),
        P(("z", "c", "x", "y"), None),
        P(("z", "c", "x", "y"), None),
        P(),
        P(None, PLANE),
        P(None, PLANE),
        P(PLANE),
        P(PLANE, None),
        P(PLANE, None),
        P(PLANE),
        P(PLANE),
        P(PLANE),
    )
    return jax.shard_map(shards, mesh=fine, in_specs=placed, out_specs=P(SPAN, PLANE), check_vma=False)
```
